32 devices in a mesh: row: 16 (over z, y, core), col: 2 (over x).
Axes of the slice: x: 2, y: 2, z: 4, core: 2. Of those that a mesh axis runs over, the one named last changes fastest.
Arguments:
- start_block: float32 [4096, 256], P(('row', 'col')), may hold values from -6 to 6
- tiles: bfloat16 [16, 2, 14, 128, 128], P('row', 'col'), may hold values from -0.125 to 0.125
- tile_rows: int32 [16, 2, 14], P('row', 'col'), may hold values from -1 to 31, as said below
- tile_cols: int32 [16, 2, 14], P('row', 'col'), may hold values from -1 to 31, as said below
- bounds: float32 [3], replicated, may hold values from -2.6 to 2.6, as said below
Outputs:
- filtered: float32 [4096, 256], P(('row', 'col'))
The draws below stay inside these ranges and needn't reach their ends.
Inputs may be any that keep to these rules, and one draw needn't show every extreme that they name: Vector rows form blocks of 128 rows, one block a device, in row+col order. On the device at grid row r and grid column c, a live slot names a block row held by one of the devices (r, any column) and a block column held by one of the devices (any row, c). Live slots come first; each device has 1 to 14 live slots, and one device has exactly 14 in every draw. No block position is named twice, and the mirror of a named position is never named unless it lies on the diagonal. tile_rows and tile_cols are -1 together. `tile_cols`: same slots as tile_rows. bounds[0] < bounds[1] < bounds[2].
All inputs are finite; a program needn't handle non-finite values.
Results may differ from the reference program's by a relative error of at most 0.0042.
Values may be sent and summed in bfloat16 or wider, within the bound.
A program may use at most 64 MiB of HBM per device.

```python
import jax
import jax.numpy as jnp
from jax import lax

K = 256
TILE = 128
BLK_DEV = 1
TILES_DEV = 14
DEGREE = 4
ORDER = 4096
N_ROW = 16
N_COL = 2


def tile_pattern(key):
    base = jax.random.fold_in(key, 7)
    group_count = N_ROW * N_COL
    near_count = N_COL * BLK_DEV
    far_count = N_ROW * BLK_DEV
    positions = near_count * far_count
    shape = (N_ROW, N_COL, near_count, far_count)
    row_grid = lax.broadcasted_iota(jnp.int32, shape, 0)
    col_grid = lax.broadcasted_iota(jnp.int32, shape, 1)
    near_grid = lax.broadcasted_iota(jnp.int32, shape, 2)
    far_grid = lax.broadcasted_iota(jnp.int32, shape, 3)
    glob_i = row_grid * near_count + near_grid
    glob_j = (far_grid // BLK_DEV * N_COL + col_grid) * BLK_DEV + far_grid % BLK_DEV
    parity = (glob_i + glob_j) % 2
    keep = (glob_i == glob_j) | (glob_i < glob_j) & (parity == 0) | (glob_i > glob_j) & (parity == 1)
    upper = max(2, (1 << 30) // positions)
    flat_index = near_grid * far_count + far_grid
    scores = jax.random.randint(jax.random.fold_in(base, 1), shape, 0, upper) * positions + flat_index
    scores = jnp.where(keep, scores, -1).reshape(N_ROW, N_COL, positions)
    chosen_scores, chosen = lax.top_k(scores, TILES_DEV)
    chosen = chosen.astype(jnp.int32)
    counts = jax.random.randint(jax.random.fold_in(base, 2), (N_ROW, N_COL), TILES_DEV // 8, TILES_DEV + 1)
    full_device = jax.random.randint(jax.random.fold_in(base, 3), (), 0, group_count)
    device_ids = lax.broadcasted_iota(jnp.int32, (N_ROW, N_COL), 0) * N_COL + lax.broadcasted_iota(jnp.int32, (N_ROW, N_COL), 1)
    counts = jnp.where(device_ids == full_device, TILES_DEV, counts)
    slot_shape = (N_ROW, N_COL, TILES_DEV)
    slot_ids = lax.broadcasted_iota(jnp.int32, slot_shape, 2)
    alive = slot_ids < counts[:, :, None]
    near_sel = chosen // far_count
    far_sel = chosen % far_count
    row_slot = lax.broadcasted_iota(jnp.int32, slot_shape, 0)
    col_slot = lax.broadcasted_iota(jnp.int32, slot_shape, 1)
    glob_rows = row_slot * near_count + near_sel
    glob_cols = (far_sel // BLK_DEV * N_COL + col_slot) * BLK_DEV + far_sel % BLK_DEV
    return (jnp.where(alive, glob_rows, -1), jnp.where(alive, glob_cols, -1))


def draw_tile_rows(key, part):
    return tile_pattern(key)[0]


def draw_tile_cols(key, part):
    return tile_pattern(key)[1]


def draw_bounds(key, part):
    uniform_part = jax.random.uniform(jax.random.fold_in(key, 11), (3,), jnp.float32)
    lowest = jnp.array([-2.6, -1.2, 2.3], jnp.float32)
    spread = jnp.array([0.3, 0.4, 0.3], jnp.float32)
    return lowest + uniform_part * spread


def block_levels(key, dims, shards, smallest, high):
    def one(dim, shards_of):
        heights = jax.random.uniform(jax.random.fold_in(jax.random.fold_in(key, 6), dim), (shards_of,), jnp.float32, smallest / len(shards), high / len(shards))
        return jnp.repeat(jnp.exp(heights), dims[dim] // shards_of).reshape((-1,) + (1,) * (len(dims) - dim - 1))

    factor_of = one(*shards[0])
    for cut in shards[1:]:
        factor_of = factor_of * one(*cut)
    return factor_of


def gaussian(own_key, shape, scale, limit, pieces=(), kind=jnp.bfloat16):
    result = jax.random.normal(own_key, shape, jnp.float32) * scale
    if len(pieces) > 0:
        result = block_levels(own_key, shape, pieces, -0.22, 0.18) * result
    return jnp.clip(result, min=-limit, max=limit).astype(kind)


def setup_inputs(seed: int = 0) -> dict:
    key_list = jax.random.split(jax.random.key(seed), 6)
    return {
        "start_block": gaussian(key_list[0], (ORDER, K), 1.0, 6.0, ((0, 32),), jnp.float32),
        "tiles": gaussian(key_list[1], (N_ROW, N_COL, TILES_DEV, TILE, TILE), (TILE * 9 * TILES_DEV // (8 * BLK_DEV)) ** -0.5, 0.125, ((0, 16), (1, 2))),
        "tile_rows": draw_tile_rows(jax.random.fold_in(key_list[5], 71), 0),
        "tile_cols": draw_tile_cols(jax.random.fold_in(key_list[5], 71), 0),
        "bounds": draw_bounds(jax.random.fold_in(key_list[5], 71), 0),
    }


def apply_matrix(vectors, tiles, tile_rows, tile_cols):
    block_count = N_ROW * N_COL * BLK_DEV
    group_count = N_ROW * N_COL
    low_vectors = lax.optimization_barrier(vectors.astype(jnp.bfloat16))
    blocks_f = low_vectors.astype(jnp.float32).reshape(block_count, TILE, K)
    tile_sets = tiles.reshape(group_count, TILES_DEV, TILE, TILE)
    row_sets = tile_rows.reshape(group_count, TILES_DEV)
    col_sets = tile_cols.reshape(group_count, TILES_DEV)

    def one_group(accum, item):
        tile_mats, rows_here, cols_here = item
        tile_f = tile_mats.astype(jnp.float32)
        is_live = rows_here >= 0
        rows_safe = jnp.maximum(rows_here, 0)
        cols_safe = jnp.maximum(cols_here, 0)
        forward = jnp.einsum('txy,tyk->txk', tile_f, blocks_f[cols_safe], precision=lax.Precision.HIGHEST)
        backward = jnp.einsum('tyx,tyk->txk', tile_f, blocks_f[rows_safe], precision=lax.Precision.HIGHEST)
        accum = accum.at[jnp.where(is_live, rows_here, block_count)].add(forward, mode="drop")
        accum = accum.at[jnp.where(is_live, cols_here, block_count)].add(backward, mode="drop")
        return accum, None

    start = jnp.zeros((block_count, TILE, K), jnp.float32)
    accum, _ = lax.scan(one_group, start, (tile_sets, row_sets, col_sets))
    return accum.reshape(block_count * TILE, K)


def reference(start_block, tiles, tile_rows, tile_cols, bounds):
    half_width = (bounds[2] - bounds[1]) * 0.5
    center = (bounds[2] + bounds[1]) * 0.5
    sigma_one = half_width / (bounds[0] - center)
    previous = start_block
    current = (apply_matrix(start_block, tiles, tile_rows, tile_cols) - center * start_block) * (sigma_one / half_width)
    sigma = sigma_one
    for turn_index in range(DEGREE - 1):
        sigma_next = 1.0 / (2.0 / sigma_one - sigma)
        product = apply_matrix(current, tiles, tile_rows, tile_cols)
        following = (product - center * current) * (2.0 * sigma_next / half_width) - (sigma * sigma_next) * previous
        previous = current
        current = following
        sigma = sigma_next
    return current
```

```python
import functools

import jax
import jax.numpy as jnp
from jax import lax
from jax.experimental import pallas as pl
from jax.experimental.pallas import tpu as pltpu
from jax.sharding import PartitionSpec as P

DEGREE = 4
CHAINS = 1
MESH = pl.DeviceIdType.MESH


def kernel(
    far, near, slots, tile, width,
    rows_ref, cols_ref, bounds_ref, start_ref, tiles_ref, out_ref,
    placed, owned, mirror, window, diagonal, low, partial, arrived, mine, state,
    tile_send, tile_recv, low_send, low_recv, part_send, part_recv,
):
    chips = far // 2
    tall = far // 4
    count = far * near
    cut = width // CHAINS
    row = lax.axis_index("row")
    col = lax.axis_index("col")
    me = row * near + col
    core = row % 2
    mid = row // 2 % 2
    high = row // 4

    def spot(high_at, mid_at, core_at):
        return core_at * chips + high_at * 2 + mid_at

    def row_of(high_at, mid_at, core_at):
        return (high_at * 2 + mid_at) * 2 + core_at

    own_spot = spot(high, mid, core)

    barrier = pltpu.get_barrier_semaphore()

    def greet(step, carry):
        other = (me + step) % count
        pl.semaphore_signal(
            barrier, inc=1, device_id=(other // near, other % near), device_id_type=MESH
        )
        return carry

    lax.fori_loop(1, count, greet, 0)

    line = (1, cut)
    lowest = jnp.full(line, bounds_ref[0], jnp.float32)
    lower = jnp.full(line, bounds_ref[1], jnp.float32)
    upper = jnp.full(line, bounds_ref[2], jnp.float32)
    half_width = (upper - lower) * 0.5
    center = (upper + lower) * 0.5
    sigma_one = half_width / (lowest - center)

    def columns(chain):
        return slice(chain * cut, (chain + 1) * cut)

    for chain in range(CHAINS):
        low[0, chain, own_spot] = start_ref[:, columns(chain)].astype(jnp.bfloat16)

    for slot in range(slots):
        placed[slot] = tiles_ref[slot]
    placed[slots] = jnp.zeros((tile, tile), jnp.bfloat16)
    places = []
    for slot in range(slots):
        glob_row = rows_ref[slot]
        glob_col = cols_ref[slot]
        place = (glob_col // near) * near + (glob_row - row * near)
        places.append(jnp.where(glob_row >= 0, place, -1))

    def put(position, carry):
        chosen = jnp.int32(slots)
        for slot in range(slots):
            chosen = jnp.where(places[slot] == position, slot, chosen)
        owned[position] = placed[chosen]
        return carry

    lax.fori_loop(0, count, put, 0)
    diagonal[...] = owned[me]
    mirror[me] = diagonal[...]
    owned[me] = jnp.zeros((tile, tile), jnp.bfloat16)

    pl.semaphore_wait(barrier, count - 1)

    def send_low(step, chain, place, target_row):
        pltpu.make_async_remote_copy(
            src_ref=low.at[step, chain, place],
            dst_ref=low.at[step, chain, place],
            send_sem=low_send.at[step, chain],
            recv_sem=low_recv.at[step, chain, place],
            device_id=(target_row, col),
            device_id_type=MESH,
        ).start()

    def await_low(step, chain, place):
        here = low.at[step, chain, place]
        pltpu.make_async_copy(here, here, low_recv.at[step, chain, place]).wait()

    def begin(step, chain):
        for offset in range(1, tall):
            send_low(step, chain, own_spot, row_of((high + offset) % tall, mid, core))
        send_low(step, chain, own_spot, row_of(high, 1 - mid, core))
        send_low(step, chain, own_spot, row_of(high, mid, 1 - core))

    def forward_line(step, chain):
        for offset in range(1, tall):
            place = spot((high + offset) % tall, mid, core)
            await_low(step, chain, place)
            send_low(step, chain, place, row_of(high, 1 - mid, core))
            send_low(step, chain, place, row_of(high, mid, 1 - core))

    def forward_mid(step, chain):
        for offset in range(tall):
            place = spot((high + offset) % tall, 1 - mid, core)
            await_low(step, chain, place)
            send_low(step, chain, place, row_of(high, mid, 1 - core))

    def await_core(step, chain):
        for offset in range(tall):
            for mid_at in range(2):
                await_low(step, chain, spot((high + offset) % tall, mid_at, 1 - core))

    def send_tile(step, carry):
        other = (me + step) % count
        pltpu.make_async_remote_copy(
            src_ref=owned.at[other],
            dst_ref=mirror.at[me],
            send_sem=tile_send,
            recv_sem=tile_recv.at[row],
            device_id=(other // near, other % near),
            device_id_type=MESH,
        ).start()
        return carry

    def build(step, carry):
        source = (row + far - step) % far
        base = source * near
        group = mirror.at[pl.ds(base, near)]
        pltpu.make_async_copy(group, group, tile_recv.at[source]).wait()
        fill(source)
        return carry

    def fill(source):
        lanes = (source % 2) * chips + source // 2
        lanes = pl.ds(pl.multiple_of(lanes * tile, tile), tile)
        for near_at in range(near):
            index = source * near + near_at
            window[near_at * tile : (near_at + 1) * tile, lanes] = (
                owned[index] + mirror[index].T
            )

    def multiply(step, chain, near_at):
        total = jnp.zeros((tile, cut), jnp.float32)
        matrix = window[pl.ds(pl.multiple_of(near_at * tile, tile), tile), :]
        vectors = low[step, chain].reshape(far * tile, cut)
        return total + jnp.dot(matrix, vectors, preferred_element_type=jnp.float32)

    def product(step, chain):
        for offset in range(1, near):
            other = (col + offset) % near
            partial[step, chain, other] = multiply(step, chain, other)
            pltpu.make_async_remote_copy(
                src_ref=partial.at[step, chain, other],
                dst_ref=arrived.at[step, chain, col],
                send_sem=part_send.at[step, chain],
                recv_sem=part_recv.at[step, chain, col],
                device_id=(row, other),
                device_id_type=MESH,
            ).start()
        mine[chain] = multiply(step, chain, col) + jnp.dot(
            diagonal[...], low[step, chain, own_spot], preferred_element_type=jnp.float32
        )

    def finish(step, chain, sigma):
        total = mine[chain]
        for offset in range(1, near):
            other = (col + offset) % near
            here = arrived.at[step, chain, other]
            pltpu.make_async_copy(here, here, part_recv.at[step, chain, other]).wait()
            total = total + arrived[step, chain, other]
        where = columns(chain)
        current = start_ref[:, where] if step == 0 else state[step - 1, :, where]
        if step == 0:
            following = (total - center * current) * (sigma_one / half_width)
            sigma_next = sigma_one
        else:
            before = start_ref[:, where] if step == 1 else state[step - 2, :, where]
            sigma_next = 1.0 / (2.0 / sigma_one - sigma)
            following = (total - center * current) * (
                2.0 * sigma_next / half_width
            ) - (sigma * sigma_next) * before
        if step == DEGREE - 1:
            out_ref[:, where] = following
        else:
            low[step + 1, chain, own_spot] = following.astype(jnp.bfloat16)
            begin(step + 1, chain)
            state[step, :, where] = following
        return sigma_next

    for chain in range(CHAINS):
        begin(0, chain)
    lax.fori_loop(1, count // 2, send_tile, 0)
    for chain in range(CHAINS):
        forward_line(0, chain)
    lax.fori_loop(count // 2, count, send_tile, 0)
    for chain in range(CHAINS):
        forward_mid(0, chain)

    if near > 1:
        group = mirror.at[pl.ds(row * near, near - 1)]
        pltpu.make_async_copy(group, group, tile_recv.at[row]).wait()
    fill(row)
    lax.fori_loop(1, far, build, 0)

    sigma = sigma_one
    for step in range(DEGREE):
        if step > 0:
            for chain in range(CHAINS):
                forward_line(step, chain)
            for chain in range(CHAINS):
                forward_mid(step, chain)
        for chain in range(CHAINS):
            await_core(step, chain)
            product(step, chain)
        for chain in range(CHAINS):
            sigma_after = finish(step, chain, sigma)
        sigma = sigma_after

    group = owned.at[pl.ds(0, count - 1)]
    pltpu.make_async_copy(group, group, tile_send).wait()
    for step in range(DEGREE):
        for chain in range(CHAINS):
            group = low.at[step, chain, pl.ds(0, far - 1)]
            pltpu.make_async_copy(group, group, low_send.at[step, chain]).wait()
            if near > 1:
                group = partial.at[step, chain, pl.ds(0, near - 1)]
                pltpu.make_async_copy(group, group, part_send.at[step, chain]).wait()


def local(start_block, tiles, tile_rows, tile_cols, bounds):
    tall, width = start_block.shape
    tile = tiles.shape[-1]
    slots = tiles.shape[2]
    far = lax.axis_size("row")
    near = lax.axis_size("col")
    assert tall == tile and far % 4 == 0
    count = far * near
    cut = width // CHAINS
    smem = pl.BlockSpec(memory_space=pltpu.SMEM)
    vmem = pl.BlockSpec(memory_space=pltpu.VMEM)
    return pl.pallas_call(
        functools.partial(kernel, far, near, slots, tile, width),
        out_shape=jax.ShapeDtypeStruct((tall, width), jnp.float32),
        in_specs=[smem, smem, smem, vmem, vmem],
        out_specs=vmem,
        scratch_shapes=[
            pltpu.VMEM((slots + 1, tile, tile), jnp.bfloat16),
            pltpu.VMEM((count, tile, tile), jnp.bfloat16),
            pltpu.VMEM((count, tile, tile), jnp.bfloat16),
            pltpu.VMEM((near * tile, far * tile), jnp.bfloat16),
            pltpu.VMEM((tile, tile), jnp.bfloat16),
            pltpu.VMEM((DEGREE, CHAINS, far, tile, cut), jnp.bfloat16),
            pltpu.VMEM((DEGREE, CHAINS, near, tile, cut), jnp.float32),
            pltpu.VMEM((DEGREE, CHAINS, near, tile, cut), jnp.float32),
            pltpu.VMEM((CHAINS, tile, cut), jnp.float32),
            pltpu.VMEM((DEGREE, tile, width), jnp.float32),
            pltpu.SemaphoreType.DMA(()),
            pltpu.SemaphoreType.DMA((far,)),
            pltpu.SemaphoreType.DMA((DEGREE, CHAINS)),
            pltpu.SemaphoreType.DMA((DEGREE, CHAINS, far)),
            pltpu.SemaphoreType.DMA((DEGREE, CHAINS)),
            pltpu.SemaphoreType.DMA((DEGREE, CHAINS, near)),
        ],
        compiler_params=pltpu.CompilerParams(
            collective_id=0, has_side_effects=True, vmem_limit_bytes=60 * 1024 * 1024
        ),
    )(
        tile_rows.reshape(slots),
        tile_cols.reshape(slots),
        bounds,
        start_block,
        tiles.reshape(slots, tile, tile),
    )


def solution(mesh):
    placed = (
        P(("row", "col"), None),
        P("row", "col", None, None, None),
        P("row", "col", None),
        P("row", "col", None),
        P(),
    )
    return jax.shard_map(
        local, mesh=mesh, in_specs=placed, out_specs=P(("row", "col"), None), check_vma=False
    )
```

```python
import functools

import jax
import jax.numpy as jnp
from jax import lax
from jax.experimental import pallas as pl
from jax.experimental.pallas import tpu as pltpu
from jax.sharding import PartitionSpec as P

DEGREE = 4
CHAINS = 2
LAG = 0
MESH = pl.DeviceIdType.MESH


def kernel(
    far, near, slots, tile, width,
    rows_ref, cols_ref, bounds_ref, start_ref, tiles_ref, out_ref,
    placed, owned, mirror, window, diagonal, low, partial, arrived, mine, state,
    tile_send, tile_recv, low_send, low_recv, part_send, part_recv,
):
    chips = far // 2
    tall = far // 4
    count = far * near
    cut = width // CHAINS
    row = lax.axis_index("row")
    col = lax.axis_index("col")
    me = row * near + col
    core = row % 2
    mid = row // 2 % 2
    high = row // 4

    def spot(high_at, mid_at, core_at):
        return core_at * chips + high_at * 2 + mid_at

    def row_of(high_at, mid_at, core_at):
        return (high_at * 2 + mid_at) * 2 + core_at

    own_spot = spot(high, mid, core)

    barrier = pltpu.get_barrier_semaphore()

    def greet(step, carry):
        other = (me + step) % count
        pl.semaphore_signal(
            barrier, inc=1, device_id=(other // near, other % near), device_id_type=MESH
        )
        return carry

    lax.fori_loop(1, count, greet, 0)

    line = (1, cut)
    lowest = jnp.full(line, bounds_ref[0], jnp.float32)
    lower = jnp.full(line, bounds_ref[1], jnp.float32)
    upper = jnp.full(line, bounds_ref[2], jnp.float32)
    half_width = (upper - lower) * 0.5
    center = (upper + lower) * 0.5
    sigma_one = half_width / (lowest - center)

    def columns(chain):
        return slice(chain * cut, (chain + 1) * cut)

    for chain in range(CHAINS):
        low[0, chain, own_spot] = start_ref[:, columns(chain)].astype(jnp.bfloat16)

    for slot in range(slots):
        placed[slot] = tiles_ref[slot]
    placed[slots] = jnp.zeros((tile, tile), jnp.bfloat16)
    places = []
    for slot in range(slots):
        glob_row = rows_ref[slot]
        glob_col = cols_ref[slot]
        place = (glob_col // near) * near + (glob_row - row * near)
        places.append(jnp.where(glob_row >= 0, place, -1))

    def put(position, carry):
        chosen = jnp.int32(slots)
        for slot in range(slots):
            chosen = jnp.where(places[slot] == position, slot, chosen)
        owned[position] = placed[chosen]
        return carry

    lax.fori_loop(0, count, put, 0)
    diagonal[...] = owned[me]
    mirror[me] = diagonal[...]
    owned[me] = jnp.zeros((tile, tile), jnp.bfloat16)

    pl.semaphore_wait(barrier, count - 1)

    flip = high >= tall // 2
    near_end = jnp.where(flip, tall - 1 - high, high)

    def along(position):
        return jnp.where(flip, tall - 1 - position, position)

    def ranked(index):
        return index + jnp.where(index >= near_end, 1, 0)

    def send_low(step, chain, place, target_row):
        pltpu.make_async_remote_copy(
            src_ref=low.at[step, chain, place],
            dst_ref=low.at[step, chain, place],
            send_sem=low_send.at[step, chain],
            recv_sem=low_recv.at[step, chain, place],
            device_id=(target_row, col),
            device_id_type=MESH,
        ).start()

    def await_low(step, chain, place):
        here = low.at[step, chain, place]
        pltpu.make_async_copy(here, here, low_recv.at[step, chain, place]).wait()

    def begin(step, chain):
        send_low(step, chain, own_spot, row_of(high, 1 - mid, core))
        for index in range(tall - 1):
            send_low(step, chain, own_spot, row_of(along(ranked(index)), mid, core))
        send_low(step, chain, own_spot, row_of(high, mid, 1 - core))

    def forward_line(step, chain):
        for index in range(tall - 1):
            place = spot(along(ranked(index)), mid, core)
            await_low(step, chain, place)
            send_low(step, chain, place, row_of(high, 1 - mid, core))
            send_low(step, chain, place, row_of(high, mid, 1 - core))

    def forward_mid(step, chain):
        for index in range(tall):
            source = high if index == 0 else along(ranked(index - 1))
            place = spot(source, 1 - mid, core)
            await_low(step, chain, place)
            send_low(step, chain, place, row_of(high, mid, 1 - core))

    def await_core(step, chain):
        for offset in range(tall):
            for mid_at in range(2):
                await_low(step, chain, spot((high + offset) % tall, mid_at, 1 - core))

    def send_tiles(high_at):
        inner = me % (4 * near)

        def send_tile(offset, carry):
            other = high_at * (4 * near) + (inner + offset) % (4 * near)
            pltpu.make_async_remote_copy(
                src_ref=owned.at[other],
                dst_ref=mirror.at[me],
                send_sem=tile_send,
                recv_sem=tile_recv.at[row],
                device_id=(other // near, other % near),
                device_id_type=MESH,
            ).start()
            return carry

        return send_tile

    def send_group(index):
        if index < 0:
            lax.fori_loop(1, 4 * near, send_tiles(high), 0)
        else:
            lax.fori_loop(0, 4 * near, send_tiles(along(ranked(index))), 0)

    def build(step, carry):
        source = (row + far - step) % far
        base = source * near
        group = mirror.at[pl.ds(base, near)]
        pltpu.make_async_copy(group, group, tile_recv.at[source]).wait()
        fill(source)
        return carry

    def fill(source):
        lanes = (source % 2) * chips + source // 2
        lanes = pl.ds(pl.multiple_of(lanes * tile, tile), tile)
        for near_at in range(near):
            index = source * near + near_at
            window[near_at * tile : (near_at + 1) * tile, lanes] = (
                owned[index] + mirror[index].T
            )

    def multiply(step, chain, near_at):
        total = jnp.zeros((tile, cut), jnp.float32)
        matrix = window[pl.ds(pl.multiple_of(near_at * tile, tile), tile), :]
        vectors = low[step, chain].reshape(far * tile, cut)
        return total + jnp.dot(matrix, vectors, preferred_element_type=jnp.float32)

    def product(step, chain):
        for offset in range(1, near):
            other = (col + offset) % near
            partial[step, chain, other] = multiply(step, chain, other)
            pltpu.make_async_remote_copy(
                src_ref=partial.at[step, chain, other],
                dst_ref=arrived.at[step, chain, col],
                send_sem=part_send.at[step, chain],
                recv_sem=part_recv.at[step, chain, col],
                device_id=(row, other),
                device_id_type=MESH,
            ).start()
        mine[chain] = multiply(step, chain, col) + jnp.dot(
            diagonal[...], low[step, chain, own_spot], preferred_element_type=jnp.float32
        )

    def finish(step, chain, sigma):
        total = mine[chain]
        for offset in range(1, near):
            other = (col + offset) % near
            here = arrived.at[step, chain, other]
            pltpu.make_async_copy(here, here, part_recv.at[step, chain, other]).wait()
            total = total + arrived[step, chain, other]
        where = columns(chain)
        current = start_ref[:, where] if step == 0 else state[step - 1, :, where]
        if step == 0:
            following = (total - center * current) * (sigma_one / half_width)
            sigma_next = sigma_one
        else:
            before = start_ref[:, where] if step == 1 else state[step - 2, :, where]
            sigma_next = 1.0 / (2.0 / sigma_one - sigma)
            following = (total - center * current) * (
                2.0 * sigma_next / half_width
            ) - (sigma * sigma_next) * before
        if step == DEGREE - 1:
            out_ref[:, where] = following
        else:
            low[step + 1, chain, own_spot] = following.astype(jnp.bfloat16)
            begin(step + 1, chain)
            state[step, :, where] = following
        return sigma_next

    for chain in range(CHAINS):
        begin(0, chain)
    groups = list(range(tall - 2, -2, -1))
    for index in groups:
        send_group(index)
    for chain in range(CHAINS):
        forward_line(0, chain)
    for chain in range(CHAINS):
        forward_mid(0, chain)

    if near > 1:
        group = mirror.at[pl.ds(row * near, near - 1)]
        pltpu.make_async_copy(group, group, tile_recv.at[row]).wait()
    fill(row)
    lax.fori_loop(1, far, build, 0)

    sigmas = [sigma_one] * CHAINS

    def phase(chain, index):
        step, part = index // 4, index % 4
        if part == 0:
            forward_line(step, chain)
        elif part == 1:
            forward_mid(step, chain)
        elif part == 2:
            await_core(step, chain)
            product(step, chain)
        else:
            sigmas[chain] = finish(step, chain, sigmas[chain])

    for index in range(2, 4 * DEGREE + LAG * (CHAINS - 1)):
        for chain in range(CHAINS):
            own_index = index - LAG * chain
            if 2 <= own_index < 4 * DEGREE:
                phase(chain, own_index)

    group = owned.at[pl.ds(0, count - 1)]
    pltpu.make_async_copy(group, group, tile_send).wait()
    for step in range(DEGREE):
        for chain in range(CHAINS):
            group = low.at[step, chain, pl.ds(0, far - 1)]
            pltpu.make_async_copy(group, group, low_send.at[step, chain]).wait()
            if near > 1:
                group = partial.at[step, chain, pl.ds(0, near - 1)]
                pltpu.make_async_copy(group, group, part_send.at[step, chain]).wait()


def local(start_block, tiles, tile_rows, tile_cols, bounds):
    tall, width = start_block.shape
    tile = tiles.shape[-1]
    slots = tiles.shape[2]
    far = lax.axis_size("row")
    near = lax.axis_size("col")
    assert tall == tile and far % 4 == 0
    count = far * near
    cut = width // CHAINS
    smem = pl.BlockSpec(memory_space=pltpu.SMEM)
    vmem = pl.BlockSpec(memory_space=pltpu.VMEM)
    return pl.pallas_call(
        functools.partial(kernel, far, near, slots, tile, width),
        out_shape=jax.ShapeDtypeStruct((tall, width), jnp.float32),
        in_specs=[smem, smem, smem, vmem, vmem],
        out_specs=vmem,
        scratch_shapes=[
            pltpu.VMEM((slots + 1, tile, tile), jnp.bfloat16),
            pltpu.VMEM((count, tile, tile), jnp.bfloat16),
            pltpu.VMEM((count, tile, tile), jnp.bfloat16),
            pltpu.VMEM((near * tile, far * tile), jnp.bfloat16),
            pltpu.VMEM((tile, tile), jnp.bfloat16),
            pltpu.VMEM((DEGREE, CHAINS, far, tile, cut), jnp.bfloat16),
            pltpu.VMEM((DEGREE, CHAINS, near, tile, cut), jnp.float32),
            pltpu.VMEM((DEGREE, CHAINS, near, tile, cut), jnp.float32),
            pltpu.VMEM((CHAINS, tile, cut), jnp.float32),
            pltpu.VMEM((DEGREE, tile, width), jnp.float32),
            pltpu.SemaphoreType.DMA(()),
            pltpu.SemaphoreType.DMA((far,)),
            pltpu.SemaphoreType.DMA((DEGREE, CHAINS)),
            pltpu.SemaphoreType.DMA((DEGREE, CHAINS, far)),
            pltpu.SemaphoreType.DMA((DEGREE, CHAINS)),
            pltpu.SemaphoreType.DMA((DEGREE, CHAINS, near)),
        ],
        compiler_params=pltpu.CompilerParams(
            collective_id=0, has_side_effects=True, vmem_limit_bytes=60 * 1024 * 1024
        ),
    )(
        tile_rows.reshape(slots),
        tile_cols.reshape(slots),
        bounds,
        start_block,
        tiles.reshape(slots, tile, tile),
    )


def solution(mesh):
    placed = (
        P(("row", "col"), None),
        P("row", "col", None, None, None),
        P("row", "col", None),
        P("row", "col", None),
        P(),
    )
    return jax.shard_map(
        local, mesh=mesh, in_specs=placed, out_specs=P(("row", "col"), None), check_vma=False
    )
```
